32 devices in a mesh: gz: 2 (over core), gx: 4 (over y, x), gy: 4 (over z).
Axes of the slice: x: 2, y: 2, z: 4, core: 2. Of those that a mesh axis runs over, the one named last changes fastest.
Arguments:
- positions: float32 [128, 3, 16384], P(('gz', 'gy'), None, 'gx'), may hold values from -8 to 8
- diffusion_noise: float32 [128, 3, 16384], P(('gz', 'gy'), None, 'gx'), may hold values from -5 to 5
- base_nuclei: float32 [16, 3], replicated, may hold values from -4.15 to 4.15, as said below
- displacements: float32 [8, 16, 3], replicated, may hold values from -0.4375 to 0.4375
- charges: float32 [16], replicated, may hold values from 2 to 14
- orbital_decay: float32 [16], replicated, may hold values from 0.6 to 2
- coefficients: float32 [16], replicated, may hold values from 0.5 to 2
- weights: float32 [16384], P('gx'), may hold values from 0.5 to 2
- counts: int32 [128], P('gx'), may hold values from 1 to 128
- branch_source: int32 [128], replicated, may hold values from 0 to 127, as said below
Outputs:
- local_energy: float32 [8, 16384], P('gz', 'gx')
- energy_estimate: float32 [8], P('gz')
- new_positions: float32 [128, 3, 16384], P(('gz', 'gy'), None, 'gx')
- new_weights: float32 [16384], P('gx')
The draws below stay inside these ranges and needn't reach their ends.
Inputs may be any that keep to these rules, and one draw needn't show every extreme that they name: `branch_source`: A permutation of the blocks. Of the 32 destination blocks of each aligned group (d // 32 equal), at most 16 have sources in any one aligned group of 32 source blocks, and some pair reaches 16 for every group, as sender and as receiver. `base_nuclei`: any two nuclei lie 1.7 or more apart.
All inputs are finite; a program needn't handle non-finite values.
Results may differ from the reference program's by a relative error of at most 0.0002.
Values sent between devices are 32-bit elements; how exact they have to be, the bound alone decides.
A program may use at most 128 MiB of HBM per device.

```python
import math
import jax
import jax.numpy as jnp
from jax import lax

NE = 128
NA = 16
BLK = 128
G = 8
W = 16384
NBLK = 128
BPD = 32
CAP = 16
N_GX = 4


def draw_base_nuclei(key, part):
    atoms = jnp.arange(NA, dtype=jnp.int32)
    lattice = jnp.stack([atoms % 4, atoms // 4 % 2, atoms // 8], axis=1).astype(jnp.float32) * 2.5
    lattice = lattice - jnp.array([3.75, 1.25, 1.25], dtype=jnp.float32)
    jitter = jax.random.uniform(jax.random.fold_in(key, 11), (NA, 3), jnp.float32, -0.4, 0.4)
    return (lattice + jitter).astype(jnp.float32)


def draw_branch_source(key, part):
    key_sigma = jax.random.fold_in(key, 21)
    key_shift = jax.random.fold_in(key, 22)
    key_order = jax.random.fold_in(key, 23)
    key_slots = jax.random.fold_in(key, 24)
    peers = N_GX
    ranking = jax.random.permutation(key_sigma, peers).astype(jnp.int32) + 3
    ranking = ranking.at[peers // 2].set(0).at[0].set(1).at[1].set(2)
    sigma = jnp.argsort(ranking, stable=True).astype(jnp.int32)
    sigma_inverse = jnp.argsort(sigma).astype(jnp.int32)
    offsets = jnp.arange(peers, dtype=jnp.int32)
    filled = BPD // CAP
    amounts = jnp.where(offsets < filled, CAP, 0).astype(jnp.int32)
    if filled >= 2 and filled < peers:
        moving = jax.random.randint(key_shift, (), 0, CAP).astype(jnp.int32)
        amounts = amounts.at[filled - 1].add(-moving).at[filled].add(moving)
    offset_list = jnp.repeat(offsets, amounts, total_repeat_length=BPD)
    source_device = jnp.broadcast_to(offsets[:, None], (peers, BPD))
    destination = sigma[(sigma_inverse[source_device] + 1 + offset_list[None, :]) % peers]
    local_order = jax.vmap(lambda part_key: jax.random.permutation(part_key, BPD))(jax.random.split(key_order, peers)).astype(jnp.int32)
    source_block = source_device * BPD + local_order
    sort_keys = destination * NBLK + jax.random.permutation(key_slots, NBLK).astype(jnp.int32).reshape(peers, BPD)
    ordering = jnp.argsort(sort_keys.reshape(-1), stable=True)
    return source_block.reshape(-1)[ordering].astype(jnp.int32)


def plant(entries, own_key, least, top_value):
    longest = entries.shape.index(max(entries.shape))
    spots = []
    for shift in (0, 1):
        where = [jax.random.randint(jax.random.fold_in(own_key, axis), (), 0, length) for axis, length in enumerate(entries.shape)]
        where[longest] = (where[longest] + shift) % entries.shape[longest]
        spots.append(tuple(where))
    return entries.at[spots[0]].set(least).at[spots[1]].set(top_value)


def block_levels(own_key, extent, cuts, least, largest):
    loudness = 1.0
    for axis_at, shards_of in cuts:
        draws = jax.random.uniform(jax.random.fold_in(jax.random.fold_in(own_key, 6), axis_at), (shards_of,), jnp.float32, least / len(cuts), largest / len(cuts))
        loudness = loudness * jnp.repeat(jnp.exp(draws), extent[axis_at] // shards_of).reshape((-1,) + (1,) * (len(extent) - 1 - axis_at))
    return loudness


def normal_values(key, extent, spread, bound, cuts=(), kind=jnp.bfloat16):
    result = spread * jax.random.normal(key, extent, jnp.float32)
    if cuts:
        result = result * block_levels(key, extent, cuts, -0.22, 0.18)
    return jnp.clip(result, -bound, bound).astype(kind)


def setup_inputs(seed: int = 0) -> dict:
    streams_of = jax.random.split(jax.random.key(seed), 11)
    positions = normal_values(streams_of[0], (NE, 3, W), 2.0, 8.0, ((0, 8), (2, 4)), jnp.float32)
    diffusion_noise = normal_values(streams_of[1], (NE, 3, W), 1.0, 5.0, ((0, 8), (2, 4)), jnp.float32)
    base_nuclei = draw_base_nuclei(jax.random.fold_in(streams_of[10], 71), 0)
    displacements = normal_values(streams_of[3], (G, NA, 3), 0.03, 0.4375, (), jnp.float32)
    charges = jnp.clip(jnp.exp(jax.random.uniform(streams_of[4], (NA,), jnp.float32, math.log(2.0), math.log(14.0))), 2.0, 14.0)
    orbital_decay = jnp.clip(jnp.exp(jax.random.uniform(streams_of[5], (NA,), jnp.float32, math.log(0.6), math.log(2.0))), 0.6, 2.0)
    coefficients = jnp.clip(jnp.exp(jax.random.uniform(streams_of[6], (NA,), jnp.float32, math.log(0.5), math.log(2.0))), 0.5, 2.0)
    weights = jnp.clip(jnp.exp(math.log(2.0) - 1.3862944 * jax.random.uniform(streams_of[7], (W,), jnp.float32) ** block_levels(streams_of[7], (W,), ((0, 4),), -0.2, 0.2)), 0.5, 2.0)
    counts = plant(jax.random.randint(streams_of[8], (NBLK,), 1, BLK + 1), jax.random.fold_in(streams_of[8], 1), 1, BLK).astype(jnp.int32)
    branch_source = draw_branch_source(jax.random.fold_in(streams_of[10], 71), 0)
    return dict(positions=positions, diffusion_noise=diffusion_noise, base_nuclei=base_nuclei, displacements=displacements, charges=charges, orbital_decay=orbital_decay, coefficients=coefficients, weights=weights, counts=counts, branch_source=branch_source)


soft_square = 0.04
cusp_value = 0.5
jastrow_range = 1.0
time_step = 0.01
step_root = 0.1

def orbital_terms(coords, centers, charges, orbital_decay, coefficients):
    offsets = coords[:, None, :, :] - centers[None, :, :, None]
    square_dist = lax.optimization_barrier(jnp.sum(offsets * offsets, axis=2))
    distance = jnp.sqrt(square_dist + soft_square)
    decay = orbital_decay[None, :, None]
    orbital_part = coefficients[None, :, None] * jnp.exp(-decay * distance)
    orbital = lax.optimization_barrier(jnp.sum(orbital_part, axis=1))
    grad_orbital = lax.optimization_barrier(jnp.sum((-decay * orbital_part / distance)[:, :, None, :] * offsets, axis=1))
    lap_orbital = lax.optimization_barrier(jnp.sum(orbital_part * (decay * decay * square_dist / (distance * distance) - decay * (2.0 * distance * distance + soft_square) / (distance * distance * distance)), axis=1))
    grad_log = grad_orbital / orbital[:, None, :]
    potential = -lax.optimization_barrier(jnp.sum(charges[None, :, None] / distance, axis=1))
    return (jnp.log(orbital), grad_log, lap_orbital / orbital, potential)

def pair_terms(coords, others, coord_index, other_index):
    offsets = coords[:, None, :, :] - others[None, :, :, :]
    square_dist = lax.optimization_barrier(jnp.sum(offsets * offsets, axis=2))
    distance = jnp.sqrt(square_dist + soft_square)
    keeping = (coord_index[:, None] != other_index[None, :]).astype(jnp.float32)[:, :, None]
    denominator = 1.0 + jastrow_range * distance
    slope = keeping * cusp_value / (denominator * denominator)
    bending = keeping * (-2.0 * cusp_value * jastrow_range) / (denominator * denominator * denominator)
    gradient = lax.optimization_barrier(jnp.sum((slope / distance)[:, :, None, :] * offsets, axis=1))
    laplacian = lax.optimization_barrier(jnp.sum(bending * square_dist / (distance * distance) + slope * (2.0 * distance * distance + soft_square) / (distance * distance * distance), axis=1))
    coulomb = 0.5 * lax.optimization_barrier(jnp.sum(keeping / distance, axis=1))
    return (gradient, laplacian, coulomb)

def nuclear_repulsion(centers, charges):
    offsets = centers[:, None, :] - centers[None, :, :]
    identity = jnp.eye(centers.shape[0], dtype=jnp.float32)
    distance = jnp.sqrt(lax.optimization_barrier(jnp.sum(offsets * offsets, axis=2)) + identity)
    return 0.5 * jnp.sum(charges[:, None] * charges[None, :] * (1.0 - identity) / distance)

def electron_energy(grad_log, laplace_ratio, potential, jgrad, jlap, coulomb):
    total_grad = grad_log + jgrad
    kinetic = -0.5 * (laplace_ratio - lax.optimization_barrier(jnp.sum(grad_log * grad_log, axis=1)) + jlap + lax.optimization_barrier(jnp.sum(total_grad * total_grad, axis=1)))
    return kinetic + potential + coulomb

def reference(positions, diffusion_noise, base_nuclei, displacements, charges, orbital_decay, coefficients, weights, counts, branch_source):
    centers = base_nuclei[None, :, :] + displacements
    block_coords = positions.reshape(NE, 3, NBLK, BLK).transpose(2, 0, 1, 3)
    electron_index = jnp.arange(NE, dtype=jnp.int32)

    def walker_block(coords):
        jgrad, jlap, coulomb = pair_terms(coords, coords, electron_index, electron_index)
        energies = []
        log_sums = []
        drifted = coords
        for geometry in range(G):
            log_orbital, grad_log, laplace_ratio, potential = orbital_terms(coords, centers[geometry], charges, orbital_decay, coefficients)
            energies.append(lax.optimization_barrier(jnp.sum(electron_energy(grad_log, laplace_ratio, potential, jgrad, jlap, coulomb), axis=0)))
            log_sums.append(lax.optimization_barrier(jnp.sum(log_orbital, axis=0)))
            if geometry == 0:
                drifted = coords + time_step * (grad_log + jgrad)
        return (jnp.stack(energies), jnp.stack(log_sums), drifted)
    energy_blocks, log_blocks, drift_blocks = lax.map(walker_block, block_coords)
    energies = energy_blocks.transpose(1, 0, 2).reshape(G, W)
    log_sums = log_blocks.transpose(1, 0, 2).reshape(G, W)
    drifted = drift_blocks.transpose(1, 2, 0, 3).reshape(NE, 3, W)
    nuclear_energy = jnp.stack([nuclear_repulsion(centers[geometry], charges) for geometry in range(G)])
    local_energy = (energies + nuclear_energy[:, None]) / NE
    alive_mask = (jnp.arange(BLK, dtype=jnp.int32)[None, :] < counts[:, None]).astype(jnp.float32).reshape(W)
    weight_ratio = jnp.exp(2.0 * (log_sums - log_sums[0:1]))
    sample_weight = weights[None, :] * weight_ratio * alive_mask[None, :]
    energy_estimate = lax.optimization_barrier(jnp.sum(sample_weight * local_energy, axis=1)) / lax.optimization_barrier(jnp.sum(sample_weight, axis=1))
    kept_weights = alive_mask * weights * jnp.exp(-(local_energy[0] - energy_estimate[0]))
    moved_positions = drifted + step_root * diffusion_noise
    new_positions = moved_positions.reshape(NE, 3, NBLK, BLK)[:, :, branch_source].reshape(NE, 3, W)
    new_weights = kept_weights.reshape(NBLK, BLK)[branch_source].reshape(W)
    return (local_energy, energy_estimate, new_positions, new_weights)
```

```python
import functools
import math

import jax
import jax.numpy as jnp
from jax import lax
from jax.experimental import pallas as pl
from jax.experimental.pallas import tpu as pltpu
from jax.sharding import PartitionSpec as P

BLK = 128
NA = 16
SOFT = 0.04
TIME_STEP = 0.01
STEP_ROOT = 0.1
ROWS = 16
LOG2E = 1.4426950408889634


def orbital_rows(consts, g, rows):
    x, y, z = rows
    square = x * x + y * y + z * z
    zero = jnp.zeros_like(x)
    phi = gx = gy = gz = s_w = s_z = s_p = pot = zero
    for a in range(NA):

        def const(n):
            return consts[g, a, n : n + 1, :]

        cx, cy, cz = const(0), const(1), const(2)
        q = square + (const(3) - (x * const(8) + y * const(9) + z * const(10)))
        ri = lax.rsqrt(q)
        e = jnp.exp2(const(4) - const(5) * (q * ri))
        ze = const(6) * e
        w = ze * ri
        z2e = const(6) * ze
        phi = phi + e
        s_w = s_w + w
        gx = gx + w * cx
        gy = gy + w * cy
        gz = gz + w * cz
        s_z = s_z + z2e
        s_p = s_p + (z2e + w) * (ri * ri)
        pot = pot + const(7) * ri
    inverse = 1.0 / phi
    lap = (s_z - 2.0 * s_w - SOFT * s_p) * inverse
    grad = ((gx - x * s_w) * inverse, (gy - y * s_w) * inverse, (gz - z * s_w) * inverse)
    return jnp.log(phi), grad, lap, pot


def geometry_kernel(first, count, own, sources, consts, pos, jgrad, energy, logs):
    electrons = own * sources
    lanes = pos.shape[-1]

    def geometry(step, carry):
        g = first + step

        def slab(n, running):
            rows = [jgrad[0, 3 + c, pl.ds(n * ROWS, ROWS), :] for c in range(3)]
            jrow = [jgrad[0, c, pl.ds(n * ROWS, ROWS), :] for c in range(3)]
            log_phi, grad, lap, pot = orbital_rows(consts, g, rows)
            dot = grad[0] * jrow[0] + grad[1] * jrow[1] + grad[2] * jrow[2]
            return (running[0] + (pot - 0.5 * lap - dot), running[1] + log_phi)

        zero = jnp.zeros((ROWS, lanes), jnp.float32)
        e, l = lax.fori_loop(0, electrons // ROWS, slab, (zero, zero))
        energy[0, pl.ds(step, 1), :] = jnp.sum(e, axis=0, keepdims=True)
        logs[0, pl.ds(step, 1), :] = jnp.sum(l, axis=0, keepdims=True)
        return carry

    lax.fori_loop(0, count, geometry, 0)


def pair_kernel(own, sources, consts, pos, drift, jgrad, energy, base, twice, shifted, counter, direct):
    electrons = own * sources
    lanes = pos.shape[-1]
    groups = electrons // 8
    half = groups // 2
    for c in range(3):
        for s in range(sources):
            block = pos[s, 0, c]
            jgrad[0, 3 + c, s * own : (s + 1) * own, :] = block
            twice[c, s * own : (s + 1) * own, :] = block
        twice[c, electrons : electrons + 8, :] = twice[c, 0:8, :]
        for k in range(8):
            shifted[k, c] = twice[c, k : k + electrons, :]
    counter[...] = jnp.zeros_like(counter)
    direct[...] = jnp.zeros_like(direct)

    def interact(k, i, steps, total):
        mine = [shifted[0, c, pl.ds(pl.multiple_of(i * 8, 8), 8), :] for c in range(3)]
        acc = [direct[c, pl.ds(pl.multiple_of(i * 8, 8), 8), :] for c in range(3)]
        for m in steps:
            j = lax.rem(i + m, groups)
            at = pl.ds(pl.multiple_of(j * 8, 8), 8)
            v = [mine[c] - shifted[k, c, at, :] for c in range(3)]
            q = (v[0] * v[0] + v[1] * v[1]) + (v[2] * v[2] + SOFT)
            ri = lax.rsqrt(q)
            root = lax.rsqrt(1.0 + q * ri)
            t = root * root
            t2 = t * t
            a = t2 * ri
            total = total + (ri + (t2 * t - a) - (SOFT * (ri * ri)) * (t2 * t + 0.5 * a))
            for c in range(3):
                f = a * v[c]
                acc[c] = acc[c] + f
                counter[k, c, at, :] = counter[k, c, at, :] + f
        for c in range(3):
            direct[c, pl.ds(pl.multiple_of(i * 8, 8), 8), :] = acc[c]
        return total

    total = jnp.zeros((8, lanes), jnp.float32)
    total = lax.fori_loop(0, groups, lambda i, e: interact(0, i, range(1, half), e), total)
    total = lax.fori_loop(0, half, lambda i, e: interact(0, i, (half,), e), total)

    def shifted_groups(n, e):
        return interact(1 + n // groups, lax.rem(n, groups), range(half), e)

    total = lax.fori_loop(0, 7 * groups, shifted_groups, total)
    square = jnp.zeros((electrons, lanes), jnp.float32)
    for c in range(3):
        back = counter[0, c]
        for k in range(1, 8):
            back = back + pltpu.roll(counter[k, c], k, 0)
        value = 0.5 * (direct[c] - back)
        jgrad[0, c] = value
        square = square + value * value
    base[0] = jnp.broadcast_to(
        jnp.sum(total, axis=0, keepdims=True) - 0.5 * jnp.sum(square, axis=0, keepdims=True),
        (8, lanes),
    )
    e_sum = jnp.zeros((1, lanes), jnp.float32)

    def slab(n, e_sum):
        at = pl.ds(pl.multiple_of(n * own, own), own)
        rows = [jgrad[0, 3 + c, at, :] for c in range(3)]
        jrow = [jgrad[0, c, at, :] for c in range(3)]
        log_phi, grad, lap, pot = orbital_rows(consts, 0, rows)
        dot = grad[0] * jrow[0] + grad[1] * jrow[1] + grad[2] * jrow[2]
        for c in range(3):
            drift[n, 0, c] = TIME_STEP * (grad[c] + jrow[c])
        return (e_sum[0] + (pot - 0.5 * lap - dot), e_sum[1] + log_phi)

    zero = jnp.zeros((own, lanes), jnp.float32)
    e, l = lax.fori_loop(0, sources, slab, (zero, zero))
    energy[0, 0:1, :] = jnp.sum(e, axis=0, keepdims=True)
    energy[0, 1:2, :] = jnp.sum(l, axis=0, keepdims=True)


def pack_kernel(blocks_here, capacity, source_ref, me_ref, pos, drift, noise, sent, count):
    me = me_ref[0]
    peers = count.shape[0]
    for p in range(peers):
        count[p] = 0

    def one(d, carry):
        source = source_ref[d]
        block = source - me * blocks_here

        @pl.when((block >= 0) & (block < blocks_here))
        def _():
            peer = d // blocks_here
            slot = count[peer]
            count[peer] = slot + 1
            sent[peer * capacity + slot] = pos[block] + drift[block] + STEP_ROOT * noise[block]

        return carry

    lax.fori_loop(0, source_ref.shape[0], one, 0)


def unpack_kernel(blocks_here, capacity, source_ref, me_ref, received, out, count):
    me = me_ref[0]
    peers = count.shape[0]
    for p in range(peers):
        count[p] = 0

    def one(d, carry):
        peer = source_ref[me * blocks_here + d] // blocks_here
        slot = count[peer]
        count[peer] = slot + 1
        out[d] = received[peer * capacity + slot]
        return carry

    lax.fori_loop(0, blocks_here, one, 0)


def nuclear_repulsion(centers, charges):
    offsets = centers[:, :, None, :] - centers[:, None, :, :]
    identity = jnp.eye(centers.shape[1], dtype=jnp.float32)
    distance = jnp.sqrt(jnp.sum(offsets * offsets, axis=3) + identity)
    products = charges[:, None] * charges[None, :] * (1.0 - identity)
    return 0.5 * jnp.sum(products / distance, axis=(1, 2))


def local(
    positions,
    diffusion_noise,
    base_nuclei,
    displacements,
    charges,
    orbital_decay,
    coefficients,
    weights,
    counts,
    branch_source,
):
    own, _, walkers = positions.shape
    geometries = displacements.shape[0]
    sources = lax.axis_size(("gz", "gy"))
    peers = lax.axis_size("gx")
    electrons = own * sources
    per_replica = geometries // lax.axis_size("gz")
    blocks_here = counts.shape[0]
    mine = blocks_here // sources
    local_walkers = walkers // sources
    replica = lax.axis_index(("gz", "gy"))
    device = lax.axis_index("gx")

    def to_blocks(x):
        return x.reshape(own, 3, blocks_here, BLK).transpose(2, 1, 0, 3)

    pos_blocks = to_blocks(positions)
    noise_blocks = to_blocks(diffusion_noise)
    arrived = lax.all_to_all(pos_blocks, ("gz", "gy"), split_axis=0, concat_axis=0, tiled=True)
    arrived = arrived.reshape(sources, mine, 3, own, BLK)

    centers = base_nuclei[None, :, :] + displacements
    shape = (geometries, NA)
    per_nucleus = [
        centers[:, :, 0],
        centers[:, :, 1],
        centers[:, :, 2],
        jnp.sum(centers * centers, axis=2) + SOFT,
        jnp.broadcast_to(jnp.log2(coefficients), shape),
        jnp.broadcast_to(orbital_decay * LOG2E, shape),
        jnp.broadcast_to(orbital_decay, shape),
        jnp.broadcast_to(-charges, shape),
        2.0 * centers[:, :, 0],
        2.0 * centers[:, :, 1],
        2.0 * centers[:, :, 2],
    ]
    table = jnp.stack(per_nucleus + [jnp.zeros(shape, jnp.float32)] * 5, axis=2)
    table = jnp.broadcast_to(table[..., None], table.shape + (BLK,))

    lane_spec = pl.BlockSpec((1, 8, BLK), lambda b: (b, 0, 0))
    table_spec = pl.BlockSpec(table.shape, lambda b: (0, 0, 0, 0))
    pos_spec = pl.BlockSpec((sources, 1, 3, own, BLK), lambda b: (0, b, 0, 0, 0))
    grad_spec = pl.BlockSpec((1, 6, electrons, BLK), lambda b: (b, 0, 0, 0))
    lane_shape = jax.ShapeDtypeStruct((mine, 8, BLK), jnp.float32)
    grad_shape = jax.ShapeDtypeStruct((mine, 6, electrons, BLK), jnp.float32)
    drift, jgrad, first, base = pl.pallas_call(
        functools.partial(pair_kernel, own, sources),
        grid=(mine,),
        in_specs=[table_spec, pos_spec],
        out_specs=[pos_spec, grad_spec, lane_spec, lane_spec],
        out_shape=[
            jax.ShapeDtypeStruct(arrived.shape, jnp.float32),
            grad_shape,
            lane_shape,
            lane_shape,
        ],
        scratch_shapes=[
            pltpu.VMEM((3, electrons + 8, BLK), jnp.float32),
            pltpu.VMEM((8, 3, electrons, BLK), jnp.float32),
            pltpu.VMEM((8, 3, electrons, BLK), jnp.float32),
            pltpu.VMEM((3, electrons, BLK), jnp.float32),
        ],
        compiler_params=pltpu.CompilerParams(vmem_limit_bytes=32 * 2**20),
        cost_estimate=pl.CostEstimate(flops=100_000_000, bytes_accessed=4_000_000, transcendentals=0),
        name="pairs",
    )(table, arrived)

    def more(start, count):
        return pl.pallas_call(
            functools.partial(geometry_kernel, start, count, own, sources),
            grid=(mine,),
            in_specs=[table_spec, pos_spec, grad_spec],
            out_specs=[lane_spec, lane_spec],
            out_shape=[lane_shape, lane_shape],
            compiler_params=pltpu.CompilerParams(vmem_limit_bytes=16 * 2**20),
            cost_estimate=pl.CostEstimate(
                flops=count * 30_000_000, bytes_accessed=8_000_000, transcendentals=0
            ),
            name=f"geometries_{start}",
        )(table, arrived, jgrad)

    split = max(1, (geometries - 1) // 2)
    energy_a, log_a = more(1, split)
    energy_b, log_b = more(1 + split, geometries - 1 - split)

    drift_back = lax.all_to_all(
        drift.reshape(blocks_here, 3, own, BLK), ("gz", "gy"), split_axis=0, concat_axis=0, tiled=True
    )
    capacity = min(blocks_here, max(2, 2 * blocks_here // peers))
    me = device.astype(jnp.int32).reshape(1)
    smem = pl.BlockSpec(memory_space=pltpu.SMEM)
    vmem = pl.BlockSpec(memory_space=pltpu.VMEM)
    sent = pl.pallas_call(
        functools.partial(pack_kernel, blocks_here, capacity),
        in_specs=[smem, smem, vmem, vmem, vmem],
        out_specs=vmem,
        out_shape=jax.ShapeDtypeStruct((peers * capacity, 3, own, BLK), jnp.float32),
        scratch_shapes=[pltpu.SMEM((peers,), jnp.int32)],
        name="pack",
    )(branch_source, me, pos_blocks, drift_back, noise_blocks)
    received = lax.all_to_all(sent, "gx", split_axis=0, concat_axis=0, tiled=True)
    new_blocks = pl.pallas_call(
        functools.partial(unpack_kernel, blocks_here, capacity),
        in_specs=[smem, smem, vmem],
        out_specs=vmem,
        out_shape=jax.ShapeDtypeStruct((blocks_here, 3, own, BLK), jnp.float32),
        scratch_shapes=[pltpu.SMEM((peers,), jnp.int32)],
        name="unpack",
    )(branch_source, me, received)
    new_positions = new_blocks.transpose(2, 1, 0, 3).reshape(own, 3, walkers)

    energies = jnp.concatenate(
        [first[:, 0:1], energy_a[:, :split], energy_b[:, : geometries - 1 - split]], axis=1
    )
    log_sums = jnp.concatenate(
        [first[:, 1:2], log_a[:, :split], log_b[:, : geometries - 1 - split]], axis=1
    )
    nuclear = nuclear_repulsion(centers, charges)
    energies = (energies + base[:, 0:1] + nuclear[None, :, None]) * (1.0 / electrons)
    my_weights = lax.dynamic_slice_in_dim(weights.reshape(blocks_here, BLK), replica * mine, mine, 0)
    my_counts = lax.dynamic_slice_in_dim(counts, replica * mine, mine, 0)
    alive_weights = my_weights * (
        jnp.arange(BLK, dtype=jnp.int32)[None, :] < my_counts[:, None]
    ).astype(jnp.float32)
    omega = alive_weights[:, None, :] * jnp.exp(2.0 * (log_sums - log_sums[:, 0:1]))
    sums = jnp.concatenate([jnp.sum(omega * energies, axis=(0, 2)), jnp.sum(omega, axis=(0, 2))])
    sums = jnp.pad(sums, (0, local_walkers - 2 * geometries)).reshape(mine, 1, BLK)
    bundle = jnp.concatenate([energies, alive_weights[:, None, :], sums], axis=1)
    gathered = lax.all_gather(bundle, ("gx", "gz", "gy"), axis=0, tiled=False)
    total = jnp.sum(
        gathered[:, :, geometries + 1, :].reshape(-1, local_walkers)[:, : 2 * geometries], axis=0
    )
    estimate = total[:geometries] / total[geometries:]
    first_geometry = lax.axis_index("gz") * per_replica
    rows = gathered.reshape(peers, sources * mine, geometries + 2, BLK)
    ours = lax.dynamic_slice(
        rows, (device, 0, first_geometry, 0), (1, sources * mine, per_replica, BLK)
    )
    local_energy = ours[0].transpose(1, 0, 2).reshape(per_replica, walkers)
    kept = rows[:, :, geometries, :] * jnp.exp(estimate[0] - rows[:, :, 0, :])
    kept = kept.reshape(peers * blocks_here, BLK)
    my_sources = lax.dynamic_slice_in_dim(branch_source, device * blocks_here, blocks_here, 0)
    new_weights = jnp.take(kept, my_sources, axis=0).reshape(walkers)
    my_estimate = lax.dynamic_slice_in_dim(estimate, first_geometry, per_replica, 0)
    return (local_energy, my_estimate, new_positions, new_weights)


def solution(mesh):
    in_specs = (
        P(("gz", "gy"), None, "gx"),
        P(("gz", "gy"), None, "gx"),
        P(),
        P(),
        P(),
        P(),
        P(),
        P("gx"),
        P("gx"),
        P(),
    )
    out_specs = (P("gz", "gx"), P("gz"), P(("gz", "gy"), None, "gx"), P("gx"))
    return jax.shard_map(local, mesh=mesh, in_specs=in_specs, out_specs=out_specs, check_vma=False)
```

```python
import functools
import math

import jax
import jax.numpy as jnp
from jax import lax
from jax.experimental import pallas as pl
from jax.experimental.pallas import tpu as pltpu
from jax.sharding import PartitionSpec as P

BLK = 128
NA = 16
SOFT = 0.04
TIME_STEP = 0.01
STEP_ROOT = 0.1
ROWS = 16
SCALE = 5.0
LOG2E = 1.4426950408889634


def orbital_rows(consts, g, rows):
    x, y, z = rows
    square = x * x + y * y + z * z
    zero = jnp.zeros_like(x)
    phi = gx = gy = gz = s_w = s_z = s_p = pot = zero
    for a in range(NA):

        def const(n):
            return consts[g, a, n : n + 1, :]

        cx, cy, cz = const(0), const(1), const(2)
        q = square + (const(3) - (x * const(8) + y * const(9) + z * const(10)))
        ri = lax.rsqrt(q)
        e = jnp.exp2(const(4) - const(5) * (q * ri))
        ze = const(6) * e
        w = ze * ri
        z2e = const(6) * ze
        phi = phi + e
        s_w = s_w + w
        gx = gx + w * cx
        gy = gy + w * cy
        gz = gz + w * cz
        s_z = s_z + z2e
        s_p = s_p + (z2e + w) * (ri * ri)
        pot = pot + const(7) * ri
    inverse = 1.0 / phi
    lap = (s_z - 2.0 * s_w - SOFT * s_p) * inverse
    grad = ((gx - x * s_w) * inverse, (gy - y * s_w) * inverse, (gz - z * s_w) * inverse)
    return jnp.log(phi), grad, lap, pot


def geometry_kernel(first, count, own, sources, consts, pos, jgrad, energy, logs):
    electrons = own * sources
    lanes = pos.shape[-1]

    def geometry(step, carry):
        g = first + step

        def slab(n, running):
            rows = [jgrad[0, 3 + c, pl.ds(n * ROWS, ROWS), :] for c in range(3)]
            jrow = [jgrad[0, c, pl.ds(n * ROWS, ROWS), :] for c in range(3)]
            log_phi, grad, lap, pot = orbital_rows(consts, g, rows)
            dot = grad[0] * jrow[0] + grad[1] * jrow[1] + grad[2] * jrow[2]
            return (running[0] + (pot - 0.5 * lap - dot), running[1] + log_phi)

        zero = jnp.zeros((ROWS, lanes), jnp.float32)
        e, l = lax.fori_loop(0, electrons // ROWS, slab, (zero, zero))
        energy[0, pl.ds(step, 1), :] = jnp.sum(e, axis=0, keepdims=True)
        logs[0, pl.ds(step, 1), :] = jnp.sum(l, axis=0, keepdims=True)
        return carry

    lax.fori_loop(0, count, geometry, 0)


def pair_kernel(own, sources, consts, pos, drift, jgrad, energy, base, shifted, counter, direct):
    electrons = own * sources
    lanes = pos.shape[-1]
    groups = electrons // 8
    half = groups // 2
    tile = math.gcd(half, 4)
    extent = shifted.shape[2]
    for c in range(3):
        for s in range(sources):
            block = pos[s, 0, c]
            jgrad[0, 3 + c, s * own : (s + 1) * own, :] = block
            shifted[0, c, s * own : (s + 1) * own, :] = block * SCALE
        shifted[0, c, electrons:extent, :] = shifted[0, c, 0 : extent - electrons, :]
        for k in range(1, 8):
            shifted[k, c, 0 : extent - 8, :] = shifted[0, c, k : k + extent - 8, :]
    counter[...] = jnp.zeros_like(counter)
    direct[...] = jnp.zeros_like(direct)

    def interact(k, first, steps, totals):
        start = pl.multiple_of(first * 8, 8)
        mine = [[shifted[0, c, pl.ds(start + 8 * i, 8), :] for c in range(3)] for i in range(tile)]
        acc = [[direct[c, pl.ds(start + 8 * i, 8), :] for c in range(3)] for i in range(tile)]
        sum_ri, sum_rest = totals
        for j in range(steps[0], tile + steps[-1]):
            at = pl.ds(start + 8 * j, 8)
            other = [shifted[k, c, at, :] for c in range(3)]
            back = [counter[k, c, at, :] for c in range(3)]
            for i in range(tile):
                if j - i not in steps:
                    continue
                v = [mine[i][c] - other[c] for c in range(3)]
                q = (v[0] * v[0] + v[1] * v[1]) + (v[2] * v[2] + 1.0)
                ri = lax.rsqrt(q)
                root = lax.rsqrt(SCALE + q * ri)
                t = root * root
                t2 = t * t
                a = t2 * ri
                sum_ri = sum_ri + ri
                sum_rest = sum_rest + t2 * ((t - ri) - (ri * ri) * (t + 0.5 * ri))
                for c in range(3):
                    f = a * v[c]
                    acc[i][c] = acc[i][c] + f
                    back[c] = back[c] + f
            for c in range(3):
                counter[k, c, at, :] = back[c]
        for i in range(tile):
            for c in range(3):
                direct[c, pl.ds(start + 8 * i, 8), :] = acc[i][c]
        return sum_ri, sum_rest

    tiles = groups // tile
    zero8 = jnp.zeros((8, lanes), jnp.float32)
    totals = lax.fori_loop(
        0, tiles, lambda n, e: interact(0, n * tile, range(1, half), e), (zero8, zero8)
    )
    totals = lax.fori_loop(
        0, half // tile, lambda n, e: interact(0, n * tile, range(half, half + 1), e), totals
    )

    def shifted_groups(n, e):
        return interact(1 + n // tiles, lax.rem(n, tiles) * tile, range(half), e)

    totals = lax.fori_loop(0, 7 * tiles, shifted_groups, totals)
    total = SCALE * totals[0] + SCALE**3 * totals[1]
    square = jnp.zeros((electrons, lanes), jnp.float32)
    for c in range(3):
        back = None
        for k in range(8):
            counter[k, c, 0 : extent - electrons, :] = (
                counter[k, c, 0 : extent - electrons, :] + counter[k, c, electrons:extent, :]
            )
            part = counter[k, c, 0:electrons, :]
            back = part if k == 0 else back + pltpu.roll(part, k, 0)
        value = 0.5 * SCALE**2 * (direct[c] - back)
        jgrad[0, c] = value
        square = square + value * value
    base[0] = jnp.broadcast_to(
        jnp.sum(total, axis=0, keepdims=True) - 0.5 * jnp.sum(square, axis=0, keepdims=True),
        (8, lanes),
    )

    def slab(n, e_sum):
        at = pl.ds(pl.multiple_of(n * own, own), own)
        rows = [jgrad[0, 3 + c, at, :] for c in range(3)]
        jrow = [jgrad[0, c, at, :] for c in range(3)]
        log_phi, grad, lap, pot = orbital_rows(consts, 0, rows)
        dot = grad[0] * jrow[0] + grad[1] * jrow[1] + grad[2] * jrow[2]
        for c in range(3):
            drift[n, 0, c] = TIME_STEP * (grad[c] + jrow[c])
        return (e_sum[0] + (pot - 0.5 * lap - dot), e_sum[1] + log_phi)

    zero = jnp.zeros((own, lanes), jnp.float32)
    e, l = lax.fori_loop(0, sources, slab, (zero, zero))
    energy[0, 0:1, :] = jnp.sum(e, axis=0, keepdims=True)
    energy[0, 1:2, :] = jnp.sum(l, axis=0, keepdims=True)


def pack_kernel(blocks_here, capacity, source_ref, me_ref, pos, drift, noise, sent, count):
    me = me_ref[0]
    peers = count.shape[0]
    for p in range(peers):
        count[p] = 0

    def one(d, carry):
        source = source_ref[d]
        block = source - me * blocks_here

        @pl.when((block >= 0) & (block < blocks_here))
        def _():
            peer = d // blocks_here
            slot = count[peer]
            count[peer] = slot + 1
            sent[peer * capacity + slot] = pos[block] + drift[block] + STEP_ROOT * noise[block]

        return carry

    lax.fori_loop(0, source_ref.shape[0], one, 0)


def unpack_kernel(blocks_here, capacity, source_ref, me_ref, received, out, count):
    me = me_ref[0]
    peers = count.shape[0]
    for p in range(peers):
        count[p] = 0

    def one(d, carry):
        peer = source_ref[me * blocks_here + d] // blocks_here
        slot = count[peer]
        count[peer] = slot + 1
        out[d] = received[peer * capacity + slot]
        return carry

    lax.fori_loop(0, blocks_here, one, 0)


def exchange_kernel(group_in, all_in, group_out, all_out, group_send, group_recv, all_send, all_recv):
    nz, nx, ny = lax.axis_size("gz"), lax.axis_size("gx"), lax.axis_size("gy")
    z, x, y = lax.axis_index("gz"), lax.axis_index("gx"), lax.axis_index("gy")
    group = nz * ny
    me_in_group = z * ny + y
    me = x * group + me_in_group

    def target(offset):
        dx, rest = offset // group, offset % group
        return (
            lax.rem(z + rest // ny, nz),
            lax.rem(x + dx, nx),
            lax.rem(y + rest % ny, ny),
        )

    def where(offset):
        tz, tx, ty = target(offset)
        return {"gz": tz, "gx": tx, "gy": ty}

    def all_copy(offset):
        return pltpu.make_async_remote_copy(
            src_ref=all_in,
            dst_ref=all_out.at[me],
            send_sem=all_send.at[offset],
            recv_sem=all_recv.at[offset],
            device_id=where(offset),
            device_id_type=pl.DeviceIdType.MESH,
        )

    def group_copy(offset):
        return pltpu.make_async_remote_copy(
            src_ref=group_in.at[target(offset)[0]],
            dst_ref=group_out.at[me_in_group],
            send_sem=group_send.at[offset],
            recv_sem=group_recv.at[offset],
            device_id=where(offset),
            device_id_type=pl.DeviceIdType.MESH,
        )

    def loop(first, last, step):
        def body(n, carry):
            step(n)
            return carry

        lax.fori_loop(first, last, body, 0)

    barrier = pltpu.get_barrier_semaphore()
    loop(
        1,
        nx * group,
        lambda n: pl.semaphore_signal(
            barrier, inc=1, device_id=where(n), device_id_type=pl.DeviceIdType.MESH
        ),
    )
    pl.semaphore_wait(barrier, nx * group - 1)
    loop(1, group, lambda n: group_copy(n).start())
    loop(1, nx * group, lambda n: all_copy(n).start())
    group_out[me_in_group] = group_in[z]
    all_out[me] = all_in[...]
    loop(1, group, lambda n: group_copy(n).wait())
    loop(1, nx * group, lambda n: all_copy(n).wait())


def nuclear_repulsion(centers, charges):
    offsets = centers[:, :, None, :] - centers[:, None, :, :]
    identity = jnp.eye(centers.shape[1], dtype=jnp.float32)
    distance = jnp.sqrt(jnp.sum(offsets * offsets, axis=3) + identity)
    products = charges[:, None] * charges[None, :] * (1.0 - identity)
    return 0.5 * jnp.sum(products / distance, axis=(1, 2))


def local(
    positions,
    diffusion_noise,
    base_nuclei,
    displacements,
    charges,
    orbital_decay,
    coefficients,
    weights,
    counts,
    branch_source,
):
    own, _, walkers = positions.shape
    geometries = displacements.shape[0]
    sources = lax.axis_size(("gz", "gy"))
    peers = lax.axis_size("gx")
    electrons = own * sources
    per_replica = geometries // lax.axis_size("gz")
    blocks_here = counts.shape[0]
    mine = blocks_here // sources
    local_walkers = walkers // sources
    replica = lax.axis_index(("gz", "gy"))
    device = lax.axis_index("gx")

    def to_blocks(x):
        return x.reshape(own, 3, blocks_here, BLK).transpose(2, 1, 0, 3)

    pos_blocks = to_blocks(positions)
    noise_blocks = to_blocks(diffusion_noise)
    arrived = lax.all_to_all(pos_blocks, ("gz", "gy"), split_axis=0, concat_axis=0, tiled=True)
    arrived = arrived.reshape(sources, mine, 3, own, BLK)

    centers = base_nuclei[None, :, :] + displacements
    shape = (geometries, NA)
    per_nucleus = [
        centers[:, :, 0],
        centers[:, :, 1],
        centers[:, :, 2],
        jnp.sum(centers * centers, axis=2) + SOFT,
        jnp.broadcast_to(jnp.log2(coefficients), shape),
        jnp.broadcast_to(orbital_decay * LOG2E, shape),
        jnp.broadcast_to(orbital_decay, shape),
        jnp.broadcast_to(-charges, shape),
        2.0 * centers[:, :, 0],
        2.0 * centers[:, :, 1],
        2.0 * centers[:, :, 2],
    ]
    table = jnp.stack(per_nucleus + [jnp.zeros(shape, jnp.float32)] * 5, axis=2)
    table = jnp.broadcast_to(table[..., None], table.shape + (BLK,))

    lane_spec = pl.BlockSpec((1, 8, BLK), lambda b: (b, 0, 0))
    table_spec = pl.BlockSpec(table.shape, lambda b: (0, 0, 0, 0))
    pos_spec = pl.BlockSpec((sources, 1, 3, own, BLK), lambda b: (0, b, 0, 0, 0))
    grad_spec = pl.BlockSpec((1, 6, electrons, BLK), lambda b: (b, 0, 0, 0))
    lane_shape = jax.ShapeDtypeStruct((mine, 8, BLK), jnp.float32)
    grad_shape = jax.ShapeDtypeStruct((mine, 6, electrons, BLK), jnp.float32)
    drift, jgrad, first, base = pl.pallas_call(
        functools.partial(pair_kernel, own, sources),
        grid=(mine,),
        in_specs=[table_spec, pos_spec],
        out_specs=[pos_spec, grad_spec, lane_spec, lane_spec],
        out_shape=[
            jax.ShapeDtypeStruct(arrived.shape, jnp.float32),
            grad_shape,
            lane_shape,
            lane_shape,
        ],
        scratch_shapes=[
            pltpu.VMEM((8, 3, electrons + electrons // 2 + 8, BLK), jnp.float32),
            pltpu.VMEM((8, 3, electrons + electrons // 2 + 8, BLK), jnp.float32),
            pltpu.VMEM((3, electrons, BLK), jnp.float32),
        ],
        compiler_params=pltpu.CompilerParams(vmem_limit_bytes=32 * 2**20),
        cost_estimate=pl.CostEstimate(flops=100_000_000, bytes_accessed=4_000_000, transcendentals=0),
        name="pairs",
    )(table, arrived)

    def more(start, count, jgrad):
        return pl.pallas_call(
            functools.partial(geometry_kernel, start, count, own, sources),
            grid=(mine,),
            in_specs=[table_spec, pos_spec, grad_spec],
            out_specs=[lane_spec, lane_spec],
            out_shape=[lane_shape, lane_shape],
            compiler_params=pltpu.CompilerParams(vmem_limit_bytes=16 * 2**20),
            cost_estimate=pl.CostEstimate(
                flops=count * 30_000_000, bytes_accessed=8_000_000, transcendentals=0
            ),
            name=f"geometries_{start}",
        )(table, arrived, jgrad)

    split = max(1, (geometries - 1) // 2)
    energy_a, log_a = more(1, split, jgrad)

    drift_back = lax.all_to_all(
        drift.reshape(blocks_here, 3, own, BLK), ("gz", "gy"), split_axis=0, concat_axis=0, tiled=True
    )
    capacity = min(blocks_here, max(2, 2 * blocks_here // peers))
    me = device.astype(jnp.int32).reshape(1)
    smem = pl.BlockSpec(memory_space=pltpu.SMEM)
    vmem = pl.BlockSpec(memory_space=pltpu.VMEM)
    sent = pl.pallas_call(
        functools.partial(pack_kernel, blocks_here, capacity),
        in_specs=[smem, smem, vmem, vmem, vmem],
        out_specs=vmem,
        out_shape=jax.ShapeDtypeStruct((peers * capacity, 3, own, BLK), jnp.float32),
        scratch_shapes=[pltpu.SMEM((peers,), jnp.int32)],
        name="pack",
    )(branch_source, me, pos_blocks, drift_back, noise_blocks)
    jgrad_later, sent = lax.optimization_barrier((jgrad, sent))
    energy_b, log_b = more(1 + split, geometries - 1 - split, jgrad_later)
    received = lax.all_to_all(sent, "gx", split_axis=0, concat_axis=0, tiled=True)
    new_blocks = pl.pallas_call(
        functools.partial(unpack_kernel, blocks_here, capacity),
        in_specs=[smem, smem, vmem],
        out_specs=vmem,
        out_shape=jax.ShapeDtypeStruct((blocks_here, 3, own, BLK), jnp.float32),
        scratch_shapes=[pltpu.SMEM((peers,), jnp.int32)],
        name="unpack",
    )(branch_source, me, received)
    new_positions = new_blocks.transpose(2, 1, 0, 3).reshape(own, 3, walkers)

    energies = jnp.concatenate(
        [first[:, 0:1], energy_a[:, :split], energy_b[:, : geometries - 1 - split]], axis=1
    )
    log_sums = jnp.concatenate(
        [first[:, 1:2], log_a[:, :split], log_b[:, : geometries - 1 - split]], axis=1
    )
    nuclear = nuclear_repulsion(centers, charges)
    energies = (energies + base[:, 0:1] + nuclear[None, :, None]) * (1.0 / electrons)
    my_weights = lax.dynamic_slice_in_dim(weights.reshape(blocks_here, BLK), replica * mine, mine, 0)
    my_counts = lax.dynamic_slice_in_dim(counts, replica * mine, mine, 0)
    alive_weights = my_weights * (
        jnp.arange(BLK, dtype=jnp.int32)[None, :] < my_counts[:, None]
    ).astype(jnp.float32)
    omega = alive_weights[:, None, :] * jnp.exp(2.0 * (log_sums - log_sums[:, 0:1]))
    sums = jnp.concatenate([jnp.sum(omega * energies, axis=(0, 2)), jnp.sum(omega, axis=(0, 2))])
    sums = jnp.pad(sums, (0, local_walkers - 2 * geometries)).reshape(mine, BLK)
    rows = energies.transpose(1, 0, 2)
    replicas = lax.axis_size("gz")
    for_group = rows.reshape(replicas, per_replica * mine, BLK)
    for_all = jnp.concatenate([rows[0], alive_weights, sums, sums], axis=0)
    group_rows, all_rows = pl.pallas_call(
        exchange_kernel,
        in_specs=[vmem, vmem],
        out_specs=[vmem, vmem],
        out_shape=[
            jax.ShapeDtypeStruct((sources, per_replica * mine, BLK), jnp.float32),
            jax.ShapeDtypeStruct((peers * sources, 4 * mine, BLK), jnp.float32),
        ],
        scratch_shapes=[
            pltpu.SemaphoreType.DMA((sources,)),
            pltpu.SemaphoreType.DMA((sources,)),
            pltpu.SemaphoreType.DMA((peers * sources,)),
            pltpu.SemaphoreType.DMA((peers * sources,)),
        ],
        compiler_params=pltpu.CompilerParams(collective_id=0, has_side_effects=True),
        name="exchange",
    )(for_group, for_all)
    all_rows = all_rows.reshape(peers * sources, 4, mine, BLK)
    total = jnp.sum(
        all_rows[:, 2].reshape(peers * sources, local_walkers)[:, : 2 * geometries], axis=0
    )
    estimate = total[:geometries] / total[geometries:]
    first_geometry = lax.axis_index("gz") * per_replica
    local_energy = (
        group_rows.reshape(sources, per_replica, local_walkers)
        .transpose(1, 0, 2)
        .reshape(per_replica, walkers)
    )
    kept = all_rows[:, 1] * jnp.exp(estimate[0] - all_rows[:, 0])
    kept = kept.reshape(peers * blocks_here, BLK)
    my_sources = lax.dynamic_slice_in_dim(branch_source, device * blocks_here, blocks_here, 0)
    new_weights = jnp.take(kept, my_sources, axis=0).reshape(walkers)
    my_estimate = lax.dynamic_slice_in_dim(estimate, first_geometry, per_replica, 0)
    return (local_energy, my_estimate, new_positions, new_weights)


def solution(mesh):
    in_specs = (
        P(("gz", "gy"), None, "gx"),
        P(("gz", "gy"), None, "gx"),
        P(),
        P(),
        P(),
        P(),
        P(),
        P("gx"),
        P("gx"),
        P(),
    )
    out_specs = (P("gz", "gx"), P("gz"), P(("gz", "gy"), None, "gx"), P("gx"))
    return jax.shard_map(local, mesh=mesh, in_specs=in_specs, out_specs=out_specs, check_vma=False)
```

```python
import functools
import math

import jax
import jax.numpy as jnp
from jax import lax
from jax.experimental import pallas as pl
from jax.experimental.pallas import tpu as pltpu
from jax.sharding import PartitionSpec as P

BLK = 128
NA = 16
SOFT = 0.04
TIME_STEP = 0.01
STEP_ROOT = 0.1
ROWS = 16
SCALE = 5.0
LOG2E = 1.4426950408889634


def orbital_rows(consts, g, rows):
    x, y, z = rows
    square = x * x + y * y + z * z
    zero = jnp.zeros_like(x)
    phi = gx = gy = gz = s_w = s_z = s_p = pot = zero
    for a in range(NA):

        def const(n):
            return consts[g, a, n : n + 1, :]

        cx, cy, cz = const(0), const(1), const(2)
        q = square + (const(3) - (x * const(8) + y * const(9) + z * const(10)))
        ri = lax.rsqrt(q)
        e = jnp.exp2(const(4) - const(5) * (q * ri))
        ze = const(6) * e
        w = ze * ri
        z2e = const(6) * ze
        phi = phi + e
        s_w = s_w + w
        gx = gx + w * cx
        gy = gy + w * cy
        gz = gz + w * cz
        s_z = s_z + z2e
        s_p = s_p + (z2e + w) * (ri * ri)
        pot = pot + const(7) * ri
    inverse = 1.0 / phi
    lap = (s_z - 2.0 * s_w - SOFT * s_p) * inverse
    grad = ((gx - x * s_w) * inverse, (gy - y * s_w) * inverse, (gz - z * s_w) * inverse)
    return jnp.log(phi), grad, lap, pot


def geometry_kernel(first, count, electrons, consts, jgrad, energy, logs):
    lanes = jgrad.shape[-1]

    def geometry(step, carry):
        g = first + step

        def slab(n, running):
            rows = [jgrad[0, 3 + c, pl.ds(n * ROWS, ROWS), :] for c in range(3)]
            jrow = [jgrad[0, c, pl.ds(n * ROWS, ROWS), :] for c in range(3)]
            log_phi, grad, lap, pot = orbital_rows(consts, g, rows)
            dot = grad[0] * jrow[0] + grad[1] * jrow[1] + grad[2] * jrow[2]
            return (running[0] + (pot - 0.5 * lap - dot), running[1] + log_phi)

        zero = jnp.zeros((ROWS, lanes), jnp.float32)
        e, l = lax.fori_loop(0, electrons // ROWS, slab, (zero, zero))
        energy[0, pl.ds(step, 1), :] = jnp.sum(e, axis=0, keepdims=True)
        logs[0, pl.ds(step, 1), :] = jnp.sum(l, axis=0, keepdims=True)
        return carry

    lax.fori_loop(0, count, geometry, 0)


def pair_kernel(own, sources, consts, pos, *refs):
    drift, jgrad, energy, base, shifted, counter, direct = refs[-7:]
    electrons = own * sources
    lanes = pos.shape[-1]
    groups = electrons // 8
    half = groups // 2
    tile = math.gcd(half, 4)
    extent = shifted.shape[2]
    for c in range(3):
        for s in range(sources):
            block = pos[s, 0, c]
            jgrad[0, 3 + c, s * own : (s + 1) * own, :] = block
            shifted[0, c, s * own : (s + 1) * own, :] = block * SCALE
        shifted[0, c, electrons:extent, :] = shifted[0, c, 0 : extent - electrons, :]
        for k in range(1, 8):
            shifted[k, c, 0 : extent - 8, :] = shifted[0, c, k : k + extent - 8, :]
    counter[...] = jnp.zeros_like(counter)
    direct[...] = jnp.zeros_like(direct)

    def interact(k, first, steps, totals):
        start = pl.multiple_of(first * 8, 8)
        mine = [[shifted[0, c, pl.ds(start + 8 * i, 8), :] for c in range(3)] for i in range(tile)]
        acc = [[direct[c, pl.ds(start + 8 * i, 8), :] for c in range(3)] for i in range(tile)]
        sum_ri, sum_rest = totals
        for j in range(steps[0], tile + steps[-1]):
            at = pl.ds(start + 8 * j, 8)
            other = [shifted[k, c, at, :] for c in range(3)]
            back = [counter[k, c, at, :] for c in range(3)]
            for i in range(tile):
                if j - i not in steps:
                    continue
                v = [mine[i][c] - other[c] for c in range(3)]
                q = (v[0] * v[0] + v[1] * v[1]) + (v[2] * v[2] + 1.0)
                ri = lax.rsqrt(q)
                root = lax.rsqrt(SCALE + q * ri)
                t = root * root
                t2 = t * t
                a = t2 * ri
                sum_ri = sum_ri + ri
                sum_rest = sum_rest + t2 * ((t - ri) - (ri * ri) * (t + 0.5 * ri))
                for c in range(3):
                    f = a * v[c]
                    acc[i][c] = acc[i][c] + f
                    back[c] = back[c] + f
            for c in range(3):
                counter[k, c, at, :] = back[c]
        for i in range(tile):
            for c in range(3):
                direct[c, pl.ds(start + 8 * i, 8), :] = acc[i][c]
        return sum_ri, sum_rest

    tiles = groups // tile
    zero8 = jnp.zeros((8, lanes), jnp.float32)
    totals = lax.fori_loop(
        0, tiles, lambda n, e: interact(0, n * tile, range(1, half), e), (zero8, zero8)
    )
    totals = lax.fori_loop(
        0, half // tile, lambda n, e: interact(0, n * tile, range(half, half + 1), e), totals
    )

    def shifted_groups(n, e):
        return interact(1 + n // tiles, lax.rem(n, tiles) * tile, range(half), e)

    totals = lax.fori_loop(0, 7 * tiles, shifted_groups, totals)
    total = SCALE * totals[0] + SCALE**3 * totals[1]
    square = jnp.zeros((electrons, lanes), jnp.float32)
    for c in range(3):
        back = None
        for k in range(8):
            counter[k, c, 0 : extent - electrons, :] = (
                counter[k, c, 0 : extent - electrons, :] + counter[k, c, electrons:extent, :]
            )
            part = counter[k, c, 0:electrons, :]
            back = part if k == 0 else back + pltpu.roll(part, k, 0)
        value = 0.5 * SCALE**2 * (direct[c] - back)
        jgrad[0, c] = value
        square = square + value * value
    base[0] = jnp.broadcast_to(
        jnp.sum(total, axis=0, keepdims=True) - 0.5 * jnp.sum(square, axis=0, keepdims=True),
        (8, lanes),
    )

    def slab(n, e_sum):
        at = pl.ds(pl.multiple_of(n * own, own), own)
        rows = [jgrad[0, 3 + c, at, :] for c in range(3)]
        jrow = [jgrad[0, c, at, :] for c in range(3)]
        log_phi, grad, lap, pot = orbital_rows(consts, 0, rows)
        dot = grad[0] * jrow[0] + grad[1] * jrow[1] + grad[2] * jrow[2]
        for c in range(3):
            drift[n, 0, c] = TIME_STEP * (grad[c] + jrow[c])
        return (e_sum[0] + (pot - 0.5 * lap - dot), e_sum[1] + log_phi)

    zero = jnp.zeros((own, lanes), jnp.float32)
    e, l = lax.fori_loop(0, sources, slab, (zero, zero))
    energy[0, 0:1, :] = jnp.sum(e, axis=0, keepdims=True)
    energy[0, 1:2, :] = jnp.sum(l, axis=0, keepdims=True)


def pack_kernel(blocks_here, capacity, source_ref, me_ref, pos, drift, noise, sent, count):
    me = me_ref[0]
    peers = count.shape[0]
    for p in range(peers):
        count[p] = 0

    def one(d, carry):
        source = source_ref[d]
        block = source - me * blocks_here

        @pl.when((block >= 0) & (block < blocks_here))
        def _():
            peer = d // blocks_here
            slot = count[peer]
            count[peer] = slot + 1
            sent[peer * capacity + slot] = pos[block] + drift[block] + STEP_ROOT * noise[block]

        return carry

    lax.fori_loop(0, source_ref.shape[0], one, 0)


def unpack_kernel(blocks_here, capacity, source_ref, me_ref, received, out, count):
    me = me_ref[0]
    peers = count.shape[0]
    for p in range(peers):
        count[p] = 0

    def one(d, carry):
        peer = source_ref[me * blocks_here + d] // blocks_here
        slot = count[peer]
        count[peer] = slot + 1
        out[d] = received[peer * capacity + slot]
        return carry

    lax.fori_loop(0, blocks_here, one, 0)


def exchange_kernel(
    geometries,
    mine,
    source_ref,
    group_in,
    all_in,
    energy_out,
    estimate_out,
    weight_out,
    group_out,
    all_out,
    group_send,
    group_recv,
    all_send,
    all_recv,
):
    nz, nx, ny = lax.axis_size("gz"), lax.axis_size("gx"), lax.axis_size("gy")
    z, x, y = lax.axis_index("gz"), lax.axis_index("gx"), lax.axis_index("gy")
    group = nz * ny
    me_in_group = z * ny + y
    me = x * group + me_in_group
    blocks_here = group * mine

    def shifted_index(index, by, size):
        return index if by == 0 else lax.rem(index + by, size)

    def where(offset):
        dx, rest = offset // group, offset % group
        return {
            "gz": shifted_index(z, rest // ny, nz),
            "gx": shifted_index(x, dx, nx),
            "gy": shifted_index(y, rest % ny, ny),
        }

    barrier = pltpu.get_barrier_semaphore()
    for n in range(1, nx * group):
        pl.semaphore_signal(
            barrier, inc=1, device_id=where(n), device_id_type=pl.DeviceIdType.MESH
        )
    pl.semaphore_wait(barrier, nx * group - 1)
    copies = []
    for n in range(1, nx * group):
        copies.append(
            pltpu.make_async_remote_copy(
                src_ref=all_in,
                dst_ref=all_out.at[me],
                send_sem=all_send.at[n],
                recv_sem=all_recv.at[n],
                device_id=where(n),
                device_id_type=pl.DeviceIdType.MESH,
            )
        )
        copies[-1].start()
    for n in range(1, group):
        target = where(n)
        copies.append(
            pltpu.make_async_remote_copy(
                src_ref=group_in.at[target["gz"]],
                dst_ref=group_out.at[me_in_group],
                send_sem=group_send.at[n],
                recv_sem=group_recv.at[n],
                device_id=target,
                device_id_type=pl.DeviceIdType.MESH,
            )
        )
        copies[-1].start()
    group_out[me_in_group] = group_in[z]
    all_out[me] = all_in[...]
    for copy in copies:
        copy.wait()

    total = jnp.sum(all_out[:, 2 * mine : 4 * mine, :], axis=0)
    total = jnp.broadcast_to(total[0:1], (8, BLK))
    below = lax.broadcasted_iota(jnp.int32, (8, BLK), 1) < geometries
    weight_total = jnp.where(below, pltpu.roll(total, BLK - geometries, 1), 1.0)
    estimate = total / weight_total
    estimate_out[...] = estimate
    reference_estimate = estimate[0:1, 0:1]

    def one(d, carry):
        source = source_ref[x * blocks_here + d]
        holder, block = source // mine, source % mine
        energy = all_out[holder, pl.ds(block, 1), :]
        alive = all_out[holder, pl.ds(mine + block, 1), :]
        weight_out[pl.ds(d, 1), :] = alive * jnp.exp(reference_estimate - energy)
        return carry

    lax.fori_loop(0, blocks_here, one, 0)
    per = energy_out.shape[0]
    for p in range(group):
        for b in range(mine):
            lanes = slice((p * mine + b) * BLK, (p * mine + b + 1) * BLK)
            energy_out[:, lanes] = group_out[p, b * per : (b + 1) * per, :]


def nuclear_repulsion(centers, charges):
    offsets = centers[:, :, None, :] - centers[:, None, :, :]
    identity = jnp.eye(centers.shape[1], dtype=jnp.float32)
    distance = jnp.sqrt(jnp.sum(offsets * offsets, axis=3) + identity)
    products = charges[:, None] * charges[None, :] * (1.0 - identity)
    return 0.5 * jnp.sum(products / distance, axis=(1, 2))


def local(
    positions,
    diffusion_noise,
    base_nuclei,
    displacements,
    charges,
    orbital_decay,
    coefficients,
    weights,
    counts,
    branch_source,
):
    own, _, walkers = positions.shape
    geometries = displacements.shape[0]
    sources = lax.axis_size(("gz", "gy"))
    peers = lax.axis_size("gx")
    electrons = own * sources
    per_replica = geometries // lax.axis_size("gz")
    blocks_here = counts.shape[0]
    mine = blocks_here // sources
    local_walkers = walkers // sources
    replica = lax.axis_index(("gz", "gy"))
    device = lax.axis_index("gx")

    def to_blocks(x):
        return x.reshape(own, 3, blocks_here, BLK).transpose(2, 1, 0, 3)

    pos_blocks = to_blocks(positions)
    noise_blocks = to_blocks(diffusion_noise)
    early = 1 if mine > 1 else mine
    by_device = pos_blocks.reshape(sources, mine, 3, own, BLK)

    def spread(x):
        return lax.all_to_all(x, ("gz", "gy"), split_axis=0, concat_axis=0, tiled=True)

    arrived = spread(by_device[:, :early])
    arrived_later = spread(by_device[:, early:]) if early < mine else None

    centers = base_nuclei[None, :, :] + displacements
    shape = (geometries, NA)
    per_nucleus = [
        centers[:, :, 0],
        centers[:, :, 1],
        centers[:, :, 2],
        jnp.sum(centers * centers, axis=2) + SOFT,
        jnp.broadcast_to(jnp.log2(coefficients), shape),
        jnp.broadcast_to(orbital_decay * LOG2E, shape),
        jnp.broadcast_to(orbital_decay, shape),
        jnp.broadcast_to(-charges, shape),
        2.0 * centers[:, :, 0],
        2.0 * centers[:, :, 1],
        2.0 * centers[:, :, 2],
    ]
    table = jnp.stack(per_nucleus + [jnp.zeros(shape, jnp.float32)] * 5, axis=2)
    table = jnp.broadcast_to(table[..., None], table.shape + (BLK,))

    lane_spec = pl.BlockSpec((1, 8, BLK), lambda b: (b, 0, 0))
    table_spec = pl.BlockSpec(table.shape, lambda b: (0, 0, 0, 0))
    pos_spec = pl.BlockSpec((sources, 1, 3, own, BLK), lambda b: (0, b, 0, 0, 0))
    grad_spec = pl.BlockSpec((1, 6, electrons, BLK), lambda b: (b, 0, 0, 0))
    extent = electrons + electrons // 2 + 8

    def pairs(coords, start, *previous):
        blocks = coords.shape[1]
        lane_shape = jax.ShapeDtypeStruct((blocks, 8, BLK), jnp.float32)
        return pl.pallas_call(
            functools.partial(pair_kernel, own, sources),
            grid=(blocks,),
            in_specs=[table_spec, pos_spec] + [pl.BlockSpec(memory_space=pl.ANY)] * len(previous),
            out_specs=[
                pl.BlockSpec((sources, 1, 3, own, BLK), lambda b: (0, b + start, 0, 0, 0)),
                grad_spec,
                lane_spec,
                lane_spec,
            ],
            out_shape=[
                jax.ShapeDtypeStruct((sources, mine, 3, own, BLK), jnp.float32),
                jax.ShapeDtypeStruct((blocks, 6, electrons, BLK), jnp.float32),
                lane_shape,
                lane_shape,
            ],
            scratch_shapes=[
                pltpu.VMEM((8, 3, extent, BLK), jnp.float32),
                pltpu.VMEM((8, 3, extent, BLK), jnp.float32),
                pltpu.VMEM((3, electrons, BLK), jnp.float32),
            ],
            input_output_aliases={2: 0} if previous else {},
            compiler_params=pltpu.CompilerParams(vmem_limit_bytes=32 * 2**20),
            cost_estimate=pl.CostEstimate(
                flops=blocks * 25_000_000, bytes_accessed=blocks * 1_000_000, transcendentals=0
            ),
            name=f"pairs_{start}",
        )(table, coords, *previous)

    def more(start, count, jgrad):
        blocks = jgrad.shape[0]
        lane_shape = jax.ShapeDtypeStruct((blocks, 8, BLK), jnp.float32)
        energy, logs = pl.pallas_call(
            functools.partial(geometry_kernel, start, count, electrons),
            grid=(blocks,),
            in_specs=[table_spec, grad_spec],
            out_specs=[lane_spec, lane_spec],
            out_shape=[lane_shape, lane_shape],
            compiler_params=pltpu.CompilerParams(vmem_limit_bytes=16 * 2**20),
            cost_estimate=pl.CostEstimate(
                flops=blocks * count * 7_500_000,
                bytes_accessed=blocks * 2_000_000,
                transcendentals=0,
            ),
            name=f"geometries_{start}_{blocks}",
        )(table, jgrad)
        return energy[:, :count], logs[:, :count]

    split = max(1, geometries // 2)
    drift, jgrad, first, base = pairs(arrived, 0)
    if arrived_later is None:
        energy_a, log_a = more(1, split, jgrad)
        early_rows = None
    else:
        early_energy, early_log = more(1, geometries - 1, jgrad)
        early_rows = (
            jnp.concatenate([first[:, 0:1], early_energy], axis=1),
            jnp.concatenate([first[:, 1:2], early_log], axis=1),
            base,
        )
        arrived_later, early_rows = lax.optimization_barrier((arrived_later, early_rows))
        drift, jgrad, first, base = pairs(arrived_later, early, drift)
        energy_a, log_a = more(1, split, jgrad)

    drift_back = lax.all_to_all(
        drift.reshape(blocks_here, 3, own, BLK), ("gz", "gy"), split_axis=0, concat_axis=0, tiled=True
    )
    capacity = min(blocks_here, max(2, 2 * blocks_here // peers))
    me = device.astype(jnp.int32).reshape(1)
    smem = pl.BlockSpec(memory_space=pltpu.SMEM)
    vmem = pl.BlockSpec(memory_space=pltpu.VMEM)
    sent = pl.pallas_call(
        functools.partial(pack_kernel, blocks_here, capacity),
        in_specs=[smem, smem, vmem, vmem, vmem],
        out_specs=vmem,
        out_shape=jax.ShapeDtypeStruct((peers * capacity, 3, own, BLK), jnp.float32),
        scratch_shapes=[pltpu.SMEM((peers,), jnp.int32)],
        name="pack",
    )(branch_source, me, pos_blocks, drift_back, noise_blocks)
    jgrad_later, sent = lax.optimization_barrier((jgrad, sent))
    energy_b, log_b = more(1 + split, geometries - 1 - split, jgrad_later)
    received = lax.all_to_all(sent, "gx", split_axis=0, concat_axis=0, tiled=True)
    new_blocks = pl.pallas_call(
        functools.partial(unpack_kernel, blocks_here, capacity),
        in_specs=[smem, smem, vmem],
        out_specs=vmem,
        out_shape=jax.ShapeDtypeStruct((blocks_here, 3, own, BLK), jnp.float32),
        scratch_shapes=[pltpu.SMEM((peers,), jnp.int32)],
        name="unpack",
    )(branch_source, me, received)
    new_positions = new_blocks.transpose(2, 1, 0, 3).reshape(own, 3, walkers)

    energies = jnp.concatenate([first[:, 0:1], energy_a, energy_b], axis=1)
    log_sums = jnp.concatenate([first[:, 1:2], log_a, log_b], axis=1)
    if early_rows is not None:
        energies = jnp.concatenate([early_rows[0], energies], axis=0)
        log_sums = jnp.concatenate([early_rows[1], log_sums], axis=0)
        base = jnp.concatenate([early_rows[2], base], axis=0)
    nuclear = nuclear_repulsion(centers, charges)
    energies = (energies + base[:, 0:1] + nuclear[None, :, None]) * (1.0 / electrons)
    my_weights = lax.dynamic_slice_in_dim(weights.reshape(blocks_here, BLK), replica * mine, mine, 0)
    my_counts = lax.dynamic_slice_in_dim(counts, replica * mine, mine, 0)
    alive_weights = my_weights * (
        jnp.arange(BLK, dtype=jnp.int32)[None, :] < my_counts[:, None]
    ).astype(jnp.float32)
    omega = alive_weights[:, None, :] * jnp.exp(2.0 * (log_sums - log_sums[:, 0:1]))
    sums = jnp.concatenate([jnp.sum(omega * energies, axis=(0, 2)), jnp.sum(omega, axis=(0, 2))])
    sums = jnp.pad(sums, (0, local_walkers - 2 * geometries)).reshape(mine, BLK)
    replicas = lax.axis_size("gz")
    for_group = (
        energies.reshape(mine, replicas, per_replica, BLK)
        .transpose(1, 0, 2, 3)
        .reshape(replicas, mine * per_replica, BLK)
    )
    for_all = jnp.concatenate([energies[:, 0], alive_weights, sums, sums], axis=0)
    local_energy, estimate, new_weights = pl.pallas_call(
        functools.partial(exchange_kernel, geometries, mine),
        in_specs=[smem, vmem, vmem],
        out_specs=[vmem, vmem, vmem],
        out_shape=[
            jax.ShapeDtypeStruct((per_replica, walkers), jnp.float32),
            jax.ShapeDtypeStruct((8, BLK), jnp.float32),
            jax.ShapeDtypeStruct((blocks_here, BLK), jnp.float32),
        ],
        scratch_shapes=[
            pltpu.VMEM((sources, per_replica * mine, BLK), jnp.float32),
            pltpu.VMEM((peers * sources, 4 * mine, BLK), jnp.float32),
            pltpu.SemaphoreType.DMA((sources,)),
            pltpu.SemaphoreType.DMA((sources,)),
            pltpu.SemaphoreType.DMA((peers * sources,)),
            pltpu.SemaphoreType.DMA((peers * sources,)),
        ],
        compiler_params=pltpu.CompilerParams(collective_id=0, has_side_effects=True),
        name="exchange",
    )(branch_source, for_group, for_all)
    new_weights = new_weights.reshape(walkers)
    first_geometry = lax.axis_index("gz") * per_replica
    my_estimate = lax.dynamic_slice_in_dim(estimate[0], first_geometry, per_replica, 0)
    return (local_energy, my_estimate, new_positions, new_weights)


def solution(mesh):
    in_specs = (
        P(("gz", "gy"), None, "gx"),
        P(("gz", "gy"), None, "gx"),
        P(),
        P(),
        P(),
        P(),
        P(),
        P("gx"),
        P("gx"),
        P(),
    )
    out_specs = (P("gz", "gx"), P("gz"), P(("gz", "gy"), None, "gx"), P("gx"))
    return jax.shard_map(local, mesh=mesh, in_specs=in_specs, out_specs=out_specs, check_vma=False)
```

```python
import functools
import math

import jax
import jax.numpy as jnp
from jax import lax
from jax.experimental import pallas as pl
from jax.experimental.pallas import tpu as pltpu
from jax.sharding import PartitionSpec as P

BLK = 128
NA = 16
SOFT = 0.04
TIME_STEP = 0.01
STEP_ROOT = 0.1
ROWS = 16
SCALE = 5.0
LOG2E = 1.4426950408889634


def orbital_rows(consts, g, rows):
    x, y, z = rows
    square = x * x + y * y + z * z
    zero = jnp.zeros_like(x)
    phi = gx = gy = gz = s_w = s_z = s_p = pot = zero
    for a in range(NA):

        def const(n):
            return consts[g, a, n : n + 1, :]

        cx, cy, cz = const(0), const(1), const(2)
        q = square + (const(3) - (x * const(8) + y * const(9) + z * const(10)))
        ri = lax.rsqrt(q)
        e = jnp.exp2(const(4) - const(5) * (q * ri))
        ze = const(6) * e
        w = ze * ri
        z2e = const(6) * ze
        phi = phi + e
        s_w = s_w + w
        gx = gx + w * cx
        gy = gy + w * cy
        gz = gz + w * cz
        s_z = s_z + z2e
        s_p = s_p + (z2e + w) * (ri * ri)
        pot = pot + const(7) * ri
    inverse = 1.0 / phi
    lap = (s_z - 2.0 * s_w - SOFT * s_p) * inverse
    grad = ((gx - x * s_w) * inverse, (gy - y * s_w) * inverse, (gz - z * s_w) * inverse)
    return jnp.log(phi), grad, lap, pot


def geometry_kernel(first, count, electrons, consts, jgrad, energy, logs):
    lanes = jgrad.shape[-1]

    def geometry(step, carry):
        g = first + step

        def slab(n, running):
            rows = [jgrad[0, 3 + c, pl.ds(n * ROWS, ROWS), :] for c in range(3)]
            jrow = [jgrad[0, c, pl.ds(n * ROWS, ROWS), :] for c in range(3)]
            log_phi, grad, lap, pot = orbital_rows(consts, g, rows)
            dot = grad[0] * jrow[0] + grad[1] * jrow[1] + grad[2] * jrow[2]
            return (running[0] + (pot - 0.5 * lap - dot), running[1] + log_phi)

        zero = jnp.zeros((ROWS, lanes), jnp.float32)
        e, l = lax.fori_loop(0, electrons // ROWS, slab, (zero, zero))
        energy[0, pl.ds(step, 1), :] = jnp.sum(e, axis=0, keepdims=True)
        logs[0, pl.ds(step, 1), :] = jnp.sum(l, axis=0, keepdims=True)
        return carry

    lax.fori_loop(0, count, geometry, 0)


def pair_kernel(own, sources, consts, pos, *refs):
    drift, jgrad, energy, base, shifted, counter, direct = refs[-7:]
    electrons = own * sources
    lanes = pos.shape[-1]
    groups = electrons // 8
    half = groups // 2
    tile = math.gcd(half, 4)
    extent = shifted.shape[2]
    for c in range(3):
        for s in range(sources):
            block = pos[s, 0, c]
            jgrad[0, 3 + c, s * own : (s + 1) * own, :] = block
            shifted[0, c, s * own : (s + 1) * own, :] = block * SCALE
        shifted[0, c, electrons:extent, :] = shifted[0, c, 0 : extent - electrons, :]
        for k in range(1, 8):
            shifted[k, c, 0 : extent - 8, :] = shifted[0, c, k : k + extent - 8, :]
    counter[...] = jnp.zeros_like(counter)
    direct[...] = jnp.zeros_like(direct)

    def interact(k, first, steps, totals):
        start = pl.multiple_of(first * 8, 8)
        mine = [[shifted[0, c, pl.ds(start + 8 * i, 8), :] for c in range(3)] for i in range(tile)]
        acc = [[direct[c, pl.ds(start + 8 * i, 8), :] for c in range(3)] for i in range(tile)]
        sum_ri, sum_rest = totals
        for j in range(steps[0], tile + steps[-1]):
            at = pl.ds(start + 8 * j, 8)
            other = [shifted[k, c, at, :] for c in range(3)]
            back = [counter[k, c, at, :] for c in range(3)]
            for i in range(tile):
                if j - i not in steps:
                    continue
                v = [mine[i][c] - other[c] for c in range(3)]
                q = (v[0] * v[0] + v[1] * v[1]) + (v[2] * v[2] + 1.0)
                ri = lax.rsqrt(q)
                root = lax.rsqrt(SCALE + q * ri)
                t = root * root
                t2 = t * t
                a = t2 * ri
                sum_ri = sum_ri + ri
                sum_rest = sum_rest + t2 * ((t - ri) - (ri * ri) * (t + 0.5 * ri))
                for c in range(3):
                    f = a * v[c]
                    acc[i][c] = acc[i][c] + f
                    back[c] = back[c] + f
            for c in range(3):
                counter[k, c, at, :] = back[c]
        for i in range(tile):
            for c in range(3):
                direct[c, pl.ds(start + 8 * i, 8), :] = acc[i][c]
        return sum_ri, sum_rest

    tiles = groups // tile
    zero8 = jnp.zeros((8, lanes), jnp.float32)
    totals = lax.fori_loop(
        0, tiles, lambda n, e: interact(0, n * tile, range(1, half), e), (zero8, zero8)
    )
    totals = lax.fori_loop(
        0, half // tile, lambda n, e: interact(0, n * tile, range(half, half + 1), e), totals
    )

    def shifted_groups(n, e):
        return interact(1 + n // tiles, lax.rem(n, tiles) * tile, range(half), e)

    totals = lax.fori_loop(0, 7 * tiles, shifted_groups, totals)
    total = SCALE * totals[0] + SCALE**3 * totals[1]
    square = jnp.zeros((electrons, lanes), jnp.float32)
    for c in range(3):
        back = None
        for k in range(8):
            counter[k, c, 0 : extent - electrons, :] = (
                counter[k, c, 0 : extent - electrons, :] + counter[k, c, electrons:extent, :]
            )
            part = counter[k, c, 0:electrons, :]
            back = part if k == 0 else back + pltpu.roll(part, k, 0)
        value = 0.5 * SCALE**2 * (direct[c] - back)
        jgrad[0, c] = value
        square = square + value * value
    base[0] = jnp.broadcast_to(
        jnp.sum(total, axis=0, keepdims=True) - 0.5 * jnp.sum(square, axis=0, keepdims=True),
        (8, lanes),
    )

    def slab(n, e_sum):
        at = pl.ds(pl.multiple_of(n * own, own), own)
        rows = [jgrad[0, 3 + c, at, :] for c in range(3)]
        jrow = [jgrad[0, c, at, :] for c in range(3)]
        log_phi, grad, lap, pot = orbital_rows(consts, 0, rows)
        dot = grad[0] * jrow[0] + grad[1] * jrow[1] + grad[2] * jrow[2]
        for c in range(3):
            drift[n, 0, c] = TIME_STEP * (grad[c] + jrow[c])
        return (e_sum[0] + (pot - 0.5 * lap - dot), e_sum[1] + log_phi)

    zero = jnp.zeros((own, lanes), jnp.float32)
    e, l = lax.fori_loop(0, sources, slab, (zero, zero))
    energy[0, 0:1, :] = jnp.sum(e, axis=0, keepdims=True)
    energy[0, 1:2, :] = jnp.sum(l, axis=0, keepdims=True)


def pack_kernel(blocks_here, capacity, source_ref, me_ref, pos, drift, noise, sent, count):
    me = me_ref[0]
    peers = count.shape[0]
    for p in range(peers):
        count[p] = 0

    def one(d, carry):
        source = source_ref[d]
        block = source - me * blocks_here

        @pl.when((block >= 0) & (block < blocks_here))
        def _():
            peer = d // blocks_here
            slot = count[peer]
            count[peer] = slot + 1
            sent[peer * capacity + slot] = pos[block] + drift[block] + STEP_ROOT * noise[block]

        return carry

    lax.fori_loop(0, source_ref.shape[0], one, 0)


def unpack_kernel(blocks_here, capacity, source_ref, me_ref, received, out, count):
    me = me_ref[0]
    peers = count.shape[0]
    for p in range(peers):
        count[p] = 0

    def one(d, carry):
        peer = source_ref[me * blocks_here + d] // blocks_here
        slot = count[peer]
        count[peer] = slot + 1
        out[d] = received[peer * capacity + slot]
        return carry

    lax.fori_loop(0, blocks_here, one, 0)


def exchange_kernel(
    geometries,
    mine,
    source_ref,
    group_in,
    all_in,
    energy_out,
    estimate_out,
    weight_out,
    group_out,
    all_out,
    group_send,
    group_recv,
    all_send,
    all_recv,
):
    nz, nx, ny = lax.axis_size("gz"), lax.axis_size("gx"), lax.axis_size("gy")
    z, x, y = lax.axis_index("gz"), lax.axis_index("gx"), lax.axis_index("gy")
    group = nz * ny
    me_in_group = z * ny + y
    me = x * group + me_in_group
    blocks_here = group * mine

    def shifted_index(index, by, size):
        return index if by == 0 else lax.rem(index + by, size)

    def where(offset):
        dx, rest = offset // group, offset % group
        return {
            "gz": shifted_index(z, rest // ny, nz),
            "gx": shifted_index(x, dx, nx),
            "gy": shifted_index(y, rest % ny, ny),
        }

    barrier = pltpu.get_barrier_semaphore()
    for n in range(1, nx * group):
        pl.semaphore_signal(
            barrier, inc=1, device_id=where(n), device_id_type=pl.DeviceIdType.MESH
        )
    pl.semaphore_wait(barrier, nx * group - 1)
    copies = []
    for n in range(1, nx * group):
        copies.append(
            pltpu.make_async_remote_copy(
                src_ref=all_in,
                dst_ref=all_out.at[me],
                send_sem=all_send.at[n],
                recv_sem=all_recv.at[n],
                device_id=where(n),
                device_id_type=pl.DeviceIdType.MESH,
            )
        )
        copies[-1].start()
    for n in range(1, group):
        target = where(n)
        copies.append(
            pltpu.make_async_remote_copy(
                src_ref=group_in.at[target["gz"]],
                dst_ref=group_out.at[me_in_group],
                send_sem=group_send.at[n],
                recv_sem=group_recv.at[n],
                device_id=target,
                device_id_type=pl.DeviceIdType.MESH,
            )
        )
        copies[-1].start()
    group_out[me_in_group] = group_in[z]
    all_out[me] = all_in[...]
    for copy in copies:
        copy.wait()

    total = jnp.sum(all_out[:, 2 * mine : 4 * mine, :], axis=0)
    total = jnp.broadcast_to(total[0:1], (8, BLK))
    below = lax.broadcasted_iota(jnp.int32, (8, BLK), 1) < geometries
    weight_total = jnp.where(below, pltpu.roll(total, BLK - geometries, 1), 1.0)
    estimate = total / weight_total
    estimate_out[...] = estimate
    reference_estimate = estimate[0:1, 0:1]

    def one(d, carry):
        source = source_ref[x * blocks_here + d]
        holder, block = source // mine, source % mine
        energy = all_out[holder, pl.ds(block, 1), :]
        alive = all_out[holder, pl.ds(mine + block, 1), :]
        weight_out[pl.ds(d, 1), :] = alive * jnp.exp(reference_estimate - energy)
        return carry

    lax.fori_loop(0, blocks_here, one, 0)
    per = energy_out.shape[0]
    for p in range(group):
        for b in range(mine):
            lanes = slice((p * mine + b) * BLK, (p * mine + b + 1) * BLK)
            energy_out[:, lanes] = group_out[p, b * per : (b + 1) * per, :]


def nuclear_repulsion(centers, charges):
    offsets = centers[:, :, None, :] - centers[:, None, :, :]
    identity = jnp.eye(centers.shape[1], dtype=jnp.float32)
    distance = jnp.sqrt(jnp.sum(offsets * offsets, axis=3) + identity)
    products = charges[:, None] * charges[None, :] * (1.0 - identity)
    return 0.5 * jnp.sum(products / distance, axis=(1, 2))


def local(
    positions,
    diffusion_noise,
    base_nuclei,
    displacements,
    charges,
    orbital_decay,
    coefficients,
    weights,
    counts,
    branch_source,
):
    own, _, walkers = positions.shape
    geometries = displacements.shape[0]
    sources = lax.axis_size(("gz", "gy"))
    peers = lax.axis_size("gx")
    electrons = own * sources
    per_replica = geometries // lax.axis_size("gz")
    blocks_here = counts.shape[0]
    mine = blocks_here // sources
    local_walkers = walkers // sources
    replica = lax.axis_index(("gz", "gy"))
    device = lax.axis_index("gx")

    def to_blocks(x):
        return x.reshape(own, 3, blocks_here, BLK).transpose(2, 1, 0, 3)

    pos_blocks = to_blocks(positions)
    noise_blocks = to_blocks(diffusion_noise)
    early = 1 if mine > 1 else mine
    by_device = pos_blocks.reshape(sources, mine, 3, own, BLK)

    def spread(x):
        return lax.all_to_all(x, ("gz", "gy"), split_axis=0, concat_axis=0, tiled=True)

    arrived = spread(by_device[:, :early])
    arrived_later = spread(by_device[:, early:]) if early < mine else None

    centers = base_nuclei[None, :, :] + displacements
    shape = (geometries, NA)
    per_nucleus = [
        centers[:, :, 0],
        centers[:, :, 1],
        centers[:, :, 2],
        jnp.sum(centers * centers, axis=2) + SOFT,
        jnp.broadcast_to(jnp.log2(coefficients), shape),
        jnp.broadcast_to(orbital_decay * LOG2E, shape),
        jnp.broadcast_to(orbital_decay, shape),
        jnp.broadcast_to(-charges, shape),
        2.0 * centers[:, :, 0],
        2.0 * centers[:, :, 1],
        2.0 * centers[:, :, 2],
    ]
    table = jnp.stack(per_nucleus + [jnp.zeros(shape, jnp.float32)] * 5, axis=2)
    table = jnp.broadcast_to(table[..., None], table.shape + (BLK,))

    lane_spec = pl.BlockSpec((1, 8, BLK), lambda b: (b, 0, 0))
    table_spec = pl.BlockSpec(table.shape, lambda b: (0, 0, 0, 0))
    pos_spec = pl.BlockSpec((sources, 1, 3, own, BLK), lambda b: (0, b, 0, 0, 0))
    grad_spec = pl.BlockSpec((1, 6, electrons, BLK), lambda b: (b, 0, 0, 0))
    extent = electrons + electrons // 2 + 8

    def pairs(coords, start, *previous):
        blocks = coords.shape[1]
        lane_shape = jax.ShapeDtypeStruct((blocks, 8, BLK), jnp.float32)
        return pl.pallas_call(
            functools.partial(pair_kernel, own, sources),
            grid=(blocks,),
            in_specs=[table_spec, pos_spec] + [pl.BlockSpec(memory_space=pl.ANY)] * len(previous),
            out_specs=[
                pl.BlockSpec((sources, 1, 3, own, BLK), lambda b: (0, b + start, 0, 0, 0)),
                grad_spec,
                lane_spec,
                lane_spec,
            ],
            out_shape=[
                jax.ShapeDtypeStruct((sources, mine, 3, own, BLK), jnp.float32),
                jax.ShapeDtypeStruct((blocks, 6, electrons, BLK), jnp.float32),
                lane_shape,
                lane_shape,
            ],
            scratch_shapes=[
                pltpu.VMEM((8, 3, extent, BLK), jnp.float32),
                pltpu.VMEM((8, 3, extent, BLK), jnp.float32),
                pltpu.VMEM((3, electrons, BLK), jnp.float32),
            ],
            input_output_aliases={2: 0} if previous else {},
            compiler_params=pltpu.CompilerParams(vmem_limit_bytes=60 * 2**20),
            cost_estimate=pl.CostEstimate(
                flops=blocks * 25_000_000, bytes_accessed=blocks * 1_000_000, transcendentals=0
            ),
            name=f"pairs_{start}",
        )(table, coords, *previous)

    def more(start, count, jgrad):
        blocks = jgrad.shape[0]
        lane_shape = jax.ShapeDtypeStruct((blocks, 8, BLK), jnp.float32)
        energy, logs = pl.pallas_call(
            functools.partial(geometry_kernel, start, count, electrons),
            grid=(blocks,),
            in_specs=[table_spec, grad_spec],
            out_specs=[lane_spec, lane_spec],
            out_shape=[lane_shape, lane_shape],
            compiler_params=pltpu.CompilerParams(vmem_limit_bytes=60 * 2**20),
            cost_estimate=pl.CostEstimate(
                flops=blocks * count * 7_500_000,
                bytes_accessed=blocks * 2_000_000,
                transcendentals=0,
            ),
            name=f"geometries_{start}_{blocks}",
        )(table, jgrad)
        return energy[:, :count], logs[:, :count]

    split = max(1, geometries // 2)
    drift, jgrad, first, base = pairs(arrived, 0)
    if arrived_later is None:
        energy_a, log_a = more(1, split, jgrad)
        early_rows = None
    else:
        early_energy, early_log = more(1, geometries - 1, jgrad)
        early_rows = (
            jnp.concatenate([first[:, 0:1], early_energy], axis=1),
            jnp.concatenate([first[:, 1:2], early_log], axis=1),
            base,
        )
        arrived_later, early_rows = lax.optimization_barrier((arrived_later, early_rows))
        drift, jgrad, first, base = pairs(arrived_later, early, drift)
        energy_a, log_a = more(1, split, jgrad)

    drift_back = lax.all_to_all(
        drift.reshape(blocks_here, 3, own, BLK), ("gz", "gy"), split_axis=0, concat_axis=0, tiled=True
    )
    capacity = min(blocks_here, max(2, 2 * blocks_here // peers))
    me = device.astype(jnp.int32).reshape(1)
    smem = pl.BlockSpec(memory_space=pltpu.SMEM)
    vmem = pl.BlockSpec(memory_space=pltpu.VMEM)
    sent = pl.pallas_call(
        functools.partial(pack_kernel, blocks_here, capacity),
        in_specs=[smem, smem, vmem, vmem, vmem],
        out_specs=vmem,
        out_shape=jax.ShapeDtypeStruct((peers * capacity, 3, own, BLK), jnp.float32),
        scratch_shapes=[pltpu.SMEM((peers,), jnp.int32)],
        name="pack",
    )(branch_source, me, pos_blocks, drift_back, noise_blocks)
    jgrad_later, sent = lax.optimization_barrier((jgrad, sent))
    energy_b, log_b = more(1 + split, geometries - 1 - split, jgrad_later)
    received = lax.all_to_all(sent, "gx", split_axis=0, concat_axis=0, tiled=True)
    new_blocks = pl.pallas_call(
        functools.partial(unpack_kernel, blocks_here, capacity),
        in_specs=[smem, smem, vmem],
        out_specs=vmem,
        out_shape=jax.ShapeDtypeStruct((blocks_here, 3, own, BLK), jnp.float32),
        scratch_shapes=[pltpu.SMEM((peers,), jnp.int32)],
        name="unpack",
    )(branch_source, me, received)
    new_positions = new_blocks.transpose(2, 1, 0, 3).reshape(own, 3, walkers)

    energies = jnp.concatenate([first[:, 0:1], energy_a, energy_b], axis=1)
    log_sums = jnp.concatenate([first[:, 1:2], log_a, log_b], axis=1)
    if early_rows is not None:
        energies = jnp.concatenate([early_rows[0], energies], axis=0)
        log_sums = jnp.concatenate([early_rows[1], log_sums], axis=0)
        base = jnp.concatenate([early_rows[2], base], axis=0)
    nuclear = nuclear_repulsion(centers, charges)
    energies = (energies + base[:, 0:1] + nuclear[None, :, None]) * (1.0 / electrons)
    my_weights = lax.dynamic_slice_in_dim(weights.reshape(blocks_here, BLK), replica * mine, mine, 0)
    my_counts = lax.dynamic_slice_in_dim(counts, replica * mine, mine, 0)
    alive_weights = my_weights * (
        jnp.arange(BLK, dtype=jnp.int32)[None, :] < my_counts[:, None]
    ).astype(jnp.float32)
    omega = alive_weights[:, None, :] * jnp.exp(2.0 * (log_sums - log_sums[:, 0:1]))
    sums = jnp.concatenate([jnp.sum(omega * energies, axis=(0, 2)), jnp.sum(omega, axis=(0, 2))])
    sums = jnp.pad(sums, (0, local_walkers - 2 * geometries)).reshape(mine, BLK)
    replicas = lax.axis_size("gz")
    for_group = (
        energies.reshape(mine, replicas, per_replica, BLK)
        .transpose(1, 0, 2, 3)
        .reshape(replicas, mine * per_replica, BLK)
    )
    for_all = jnp.concatenate([energies[:, 0], alive_weights, sums, sums], axis=0)
    local_energy, estimate, new_weights = pl.pallas_call(
        functools.partial(exchange_kernel, geometries, mine),
        in_specs=[smem, vmem, vmem],
        out_specs=[vmem, vmem, vmem],
        out_shape=[
            jax.ShapeDtypeStruct((per_replica, walkers), jnp.float32),
            jax.ShapeDtypeStruct((8, BLK), jnp.float32),
            jax.ShapeDtypeStruct((blocks_here, BLK), jnp.float32),
        ],
        scratch_shapes=[
            pltpu.VMEM((sources, per_replica * mine, BLK), jnp.float32),
            pltpu.VMEM((peers * sources, 4 * mine, BLK), jnp.float32),
            pltpu.SemaphoreType.DMA((sources,)),
            pltpu.SemaphoreType.DMA((sources,)),
            pltpu.SemaphoreType.DMA((peers * sources,)),
            pltpu.SemaphoreType.DMA((peers * sources,)),
        ],
        compiler_params=pltpu.CompilerParams(collective_id=0, has_side_effects=True),
        name="exchange",
    )(branch_source, for_group, for_all)
    new_weights = new_weights.reshape(walkers)
    first_geometry = lax.axis_index("gz") * per_replica
    my_estimate = lax.dynamic_slice_in_dim(estimate[0], first_geometry, per_replica, 0)
    return (local_energy, my_estimate, new_positions, new_weights)


def solution(mesh):
    in_specs = (
        P(("gz", "gy"), None, "gx"),
        P(("gz", "gy"), None, "gx"),
        P(),
        P(),
        P(),
        P(),
        P(),
        P("gx"),
        P("gx"),
        P(),
    )
    out_specs = (P("gz", "gx"), P("gz"), P(("gz", "gy"), None, "gx"), P("gx"))
    return jax.shard_map(local, mesh=mesh, in_specs=in_specs, out_specs=out_specs, check_vma=False)
```
